32 devices in a mesh: chan: 4 (over y, x), slab: 8 (over z, core).
Axes of the slice: x: 2, y: 2, z: 4, core: 2. Of those that a mesh axis runs over, the one named last changes fastest.
Arguments:
- volume: bfloat16 [128, 16, 128, 128], P('chan', 'slab'), may hold values from -6 to 6
- weight_one: bfloat16 [3, 3, 3, 128, 256], P(None, None, None, 'chan'), may hold values from -0.125 to 0.125
- bias_one: float32 [256], replicated, may hold values from -3 to 3
- weight_two: bfloat16 [3, 3, 3, 32, 256], replicated, may hold values from -0.21875 to 0.21875
- bias_two: float32 [256], replicated, may hold values from -3 to 3
Outputs:
- activated: bfloat16 [8, 64, 64, 256], P('slab', 'chan')
- grouped: bfloat16 [8, 64, 64, 256], P('slab', 'chan')
The draws below stay inside these ranges and needn't reach their ends.
All inputs are finite; a program needn't handle non-finite values.
Results may differ from the reference program's by a relative error of at most 0.018.
Values may be sent and summed in bfloat16 or wider, within the bound.
A program may use at most 64 MiB of HBM per device.

```python
import jax
import jax.numpy as jnp
from jax import lax

CIN = 128
COUT = 256
GROUPS = 8
SIDE = 128
DEPTH = 16
N_CHAN = 4


def raised(values, stream_key, source, target, blocks, factor):
    owner, partner = [(jnp.arange(values.shape[position]) // (values.shape[position] // blocks)).reshape([-1 if axis == position else 1 for axis in range(values.ndim)]) for position in (source, target)]
    chosen = jax.random.permutation(stream_key, blocks)[partner]
    strong = (owner == chosen) | (owner == (partner + blocks // 2) % blocks)
    return jnp.where(strong, factor * values, values)


def levels(stream_key, dims, pieces, low, top_value):
    level, own = 1.0, jax.random.fold_in(stream_key, 6)
    for position, parts in pieces:
        heights = jnp.exp(jax.random.uniform(jax.random.fold_in(own, position), (parts,), jnp.float32, low / len(pieces), top_value / len(pieces)))
        level = level * jnp.repeat(heights, dims[position] // parts).reshape([-1 if axis == position else 1 for axis in range(len(dims))])
    return level


def centred(stream_key, shape, deviation, limit, split=(), dtype=jnp.bfloat16):
    array = deviation * jax.random.normal(stream_key, shape, jnp.float32)
    if split:
        array = array * levels(stream_key, shape, split, -0.22, 0.18)
    return jnp.clip(array, -limit, limit).astype(dtype)


def noise_with(own_key, shape, scale, limit, split, heavy, kind=jnp.bfloat16):
    drawn = scale * jax.random.normal(own_key, shape, jnp.float32)
    if split:
        drawn = drawn * levels(own_key, shape, split, -0.22, 0.18)
    return jnp.clip(raised(drawn, jax.random.fold_in(own_key, 3), *heavy), -limit, limit).astype(kind)


def setup_inputs(seed: int = 0) -> dict:
    arg_keys = jax.random.split(jax.random.key(seed), 6)
    return {
        "volume": centred(arg_keys[0], (CIN, DEPTH, SIDE, SIDE), 1.0, 6.0, ((0, 4), (1, 8))),
        "weight_one": noise_with(arg_keys[1], (3, 3, 3, CIN, COUT), (27 * CIN) ** -0.5, 0.125, ((3, 4),), (3, 4, 4, 2.0)),
        "bias_one": centred(arg_keys[2], (COUT,), 0.5, 3.0, (), jnp.float32),
        "weight_two": centred(arg_keys[3], (3, 3, 3, COUT // GROUPS, COUT), (27 * (COUT // GROUPS)) ** -0.5, 0.21875),
        "bias_two": centred(arg_keys[4], (COUT,), 0.5, 3.0, (), jnp.float32),
    }


def leaky(value):
    return jnp.where(value > 0, value, 0.3 * value)


def reference(volume, weight_one, bias_one, weight_two, bias_two):
    block = CIN // N_CHAN
    blocks = volume.reshape(N_CHAN, block, DEPTH, SIDE, SIDE)
    kernels = weight_one.reshape(3, 3, 3, N_CHAN, block, COUT).transpose(3, 0, 1, 2, 4, 5)

    def add_block(total, pair):
        piece, kernel = pair
        part = lax.conv_general_dilated(
            piece[None].astype(jnp.float32), kernel.astype(jnp.float32), (2, 2, 2),
            ((1, 0), (1, 0), (1, 0)), dimension_numbers=("NCDHW", "DHWIO", "NDHWC"),
            precision=lax.Precision.HIGHEST)[0]
        rounded = lax.optimization_barrier(part.astype(jnp.bfloat16))
        return total + rounded.astype(jnp.float32), None

    start = jnp.zeros((DEPTH // 2, SIDE // 2, SIDE // 2, COUT), jnp.float32)
    summed, _ = lax.scan(add_block, start, (blocks, kernels))
    activated = leaky(summed + bias_one.astype(jnp.float32)).astype(jnp.bfloat16)
    second = lax.conv_general_dilated(
        activated[None].astype(jnp.float32), weight_two.astype(jnp.float32), (1, 1, 1),
        ((1, 1), (1, 1), (1, 1)), dimension_numbers=("NDHWC", "DHWIO", "NDHWC"),
        feature_group_count=GROUPS, precision=lax.Precision.HIGHEST)[0]
    grouped = (second + bias_two.astype(jnp.float32)).astype(jnp.bfloat16)
    return activated, grouped
```

```python
import functools

import jax
import jax.numpy as jnp
from jax import lax
from jax.experimental import pallas as pl
from jax.experimental.pallas import tpu as pltpu
from jax.sharding import PartitionSpec as P

BF = jnp.bfloat16
F32 = jnp.float32
MESH = pl.DeviceIdType.MESH
AROUND = [(0, 1), (0, -1), (1, 0), (-1, 0), (1, 1), (1, -1), (-1, 1), (-1, -1)]


def leaky(value):
    return jnp.where(value > 0, value, 0.3 * value)


def body(parts, slabs, own_ref, k1_ref, b1_ref, k2_ref, b2_ref, act_ref, out_ref,
         low_ref, t_ref, part_ref, recv_ref, a_ref, w1_ref, w2_ref, acc_ref,
         low_send, low_recv, sum_send, sum_recv, halo_send, halo_recv):
    c = own_ref.shape[2]
    tall = 128 // c
    wins = own_ref.shape[1] // tall
    half = own_ref.shape[3] // 2
    mine, q, k = act_ref.shape
    outs = tall // 2
    step = 4 * outs if mine % (4 * outs) == 0 else mine
    pieces = mine // step
    me, slab = lax.axis_index("chan"), lax.axis_index("slab")

    def peer(s):
        if parts == 4:
            return 2 * lax.rem(me // 2 + lax.div(s, 2), 2) + lax.rem(lax.rem(me, 2) + lax.rem(s, 2), 2)
        return lax.rem(me + s, parts)

    def inside(dc, ds):
        ok = None
        for coord, move, size in ((me, dc, parts), (slab, ds, slabs)):
            if move:
                one = coord + move < size if move > 0 else coord + move >= 0
                ok = one if ok is None else jnp.logical_and(ok, one)
        return ok

    barrier = pltpu.get_barrier_semaphore()
    for s in range(1, parts):
        pl.semaphore_signal(barrier, inc=1, device_id={"chan": peer(jnp.int32(s)), "slab": slab}, device_id_type=MESH)
    for dc, ds in AROUND:
        if ds:
            @pl.when(inside(dc, ds))
            def _(dc=dc, ds=ds):
                pl.semaphore_signal(barrier, inc=1, device_id={"chan": me + dc, "slab": slab + ds}, device_id_type=MESH)
    one = jnp.int32(1)
    across = jnp.minimum(slab, one) + jnp.minimum(jnp.int32(slabs - 1) - slab, one)
    along = one + jnp.minimum(me, one) + jnp.minimum(jnp.int32(parts - 1) - me, one)
    pl.semaphore_wait(barrier, jnp.int32(parts - 1) + across * along)

    def low_copy():
        return pltpu.make_async_remote_copy(
            src_ref=own_ref.at[own_ref.shape[0] - 1], dst_ref=low_ref, send_sem=low_send, recv_sem=low_recv,
            device_id={"chan": me, "slab": slab + 1}, device_id_type=MESH)

    @pl.when(slab + 1 < slabs)
    def _():
        low_copy().start()

    w1_ref[...] = jnp.zeros_like(w1_ref)
    for e in range(9):
        i, l = divmod(e, 3)
        for par in range(outs):
            for j in range(3):
                start = e * 256 + (tall - 1 + 2 * par + j) * c
                w1_ref[start:start + c, par * k:(par + 1) * k] = k1_ref[i, j, l]
    m = k2_ref.shape[3]
    group = lax.broadcasted_iota(jnp.int32, (m, k), 1) // m
    for i in range(3):
        for l in range(3):
            for j in range(3):
                taps = k2_ref[i, j, l]
                for g in range(k // m):
                    w2_ref[i, l, j * k + g * m:j * k + (g + 1) * m] = jnp.where(group == g, taps, jnp.zeros_like(taps))
    width = own_ref.shape[3]
    spot = lax.broadcasted_iota(jnp.int32, (half, width), 1) - 2 * lax.broadcasted_iota(jnp.int32, (half, width), 0)
    sel = jnp.concatenate([jnp.where(spot == l - 1, 1.0, 0.0) for l in range(3)], axis=0).astype(BF)
    for e in range(9):
        t_ref[e, 0] = jnp.zeros_like(t_ref[e, 0])

    def decimate(d):
        def go(b, carry):
            rows = pl.ds(4 * tall * b, 4 * tall)
            x = low_ref[rows] if d == 0 else own_ref[d - 1, rows]
            x = x.reshape(512, own_ref.shape[3])
            t = lax.dot_general(sel, x, (((1,), (1,)), ((), ())), preferred_element_type=F32).astype(BF)
            for l in range(3):
                for u in range(4):
                    t_ref[3 * d + l, 4 * b + u + 1] = t[l * half:(l + 1) * half, 128 * u:128 * (u + 1)]
            return carry

        lax.fori_loop(0, wins // 4, go, 0)

    decimate(1)
    decimate(2)

    @pl.when(slab == 0)
    def _():
        low_ref[...] = jnp.zeros_like(low_ref)

    @pl.when(slab > 0)
    def _():
        low_copy().wait_recv()

    decimate(0)

    def chunk(b):
        lhs = []
        for e in range(9):
            lhs.append(t_ref[e, pl.ds(4 * b, 4)].reshape(4 * half, 128))
            lhs.append(t_ref[e, pl.ds(4 * b + 1, 4)].reshape(4 * half, 128))
        res = jnp.dot(jnp.concatenate(lhs, axis=1), w1_ref[...], preferred_element_type=F32).astype(BF)
        for u in range(4):
            for par in range(outs):
                part_ref[4 * outs * b + outs * u + par] = res[u * half:(u + 1) * half, par * k:(par + 1) * k]

    def sum_copy(s, h):
        to = peer(s)
        return pltpu.make_async_remote_copy(
            src_ref=part_ref.at[pl.ds(to * mine + h * step, step)], dst_ref=recv_ref.at[s - 1, pl.ds(h * step, step)],
            send_sem=sum_send.at[s - 1, h], recv_sem=sum_recv.at[s - 1, h],
            device_id={"chan": to, "slab": slab}, device_id_type=MESH)

    if step == 4 * outs:
        def one(n, carry):
            s, h = parts - 1 - lax.div(n, pieces), lax.rem(n, pieces)
            chunk(peer(s) * pieces + h)

            @pl.when(n < (parts - 1) * pieces)
            def _():
                sum_copy(s, h).start()
            return carry

        lax.fori_loop(0, parts * pieces, one, 0)
    else:
        def one(n, carry):
            chunk(n)
            return carry

        lax.fori_loop(0, wins // 4, one, 0)
        for s in range(1, parts):
            sum_copy(jnp.int32(s), 0).start()

    for h in range(pieces):
        for s in range(1, parts):
            sum_copy(jnp.int32(s), h).wait_recv()
        for r in range(h * step, (h + 1) * step, 4):
            total = part_ref[pl.ds(me * mine + r, 4)].astype(F32)
            for s in range(1, parts):
                total += recv_ref[s - 1, r:r + 4].astype(F32)
            act = leaky(total + b1_ref[...]).astype(BF)
            act_ref[r:r + 4] = act
            a_ref[1, r + 1:r + 5] = act

    def spots(dc, ds):
        if dc == 0:
            return a_ref.at[1, pl.ds(1, mine)], a_ref.at[1 - ds, pl.ds(1, mine)]
        return a_ref.at[1, pl.ds(mine if dc > 0 else 1, 1)], a_ref.at[1 - ds, pl.ds(0 if dc > 0 else mine + 1, 1)]

    def halo_copy(n):
        dc, ds = AROUND[n]
        src, dst = spots(dc, ds)
        return pltpu.make_async_remote_copy(
            src_ref=src, dst_ref=dst, send_sem=halo_send.at[n], recv_sem=halo_recv.at[n],
            device_id={"chan": me + dc, "slab": slab + ds}, device_id_type=MESH)

    def arrive(n):
        dc, ds = AROUND[n]
        there = inside(-dc, -ds)

        @pl.when(there)
        def _():
            halo_copy(n).wait_recv()

        @pl.when(jnp.logical_not(there))
        def _():
            dst = spots(dc, ds)[1]
            dst[...] = jnp.zeros(dst.shape, BF)

    for n, (dc, ds) in enumerate(AROUND):
        @pl.when(inside(dc, ds))
        def _(n=n):
            halo_copy(n).start()

    for i, last in ((1, False), (0, False), (2, True)):
        for n, (dc, ds) in enumerate(AROUND):
            if 1 - ds == i:
                arrive(n)

        def rows4(b, carry, i=i, last=last):
            lhs = jnp.concatenate([a_ref[i, pl.ds(4 * b + j, 4)].reshape(4 * q, k) for j in range(3)], axis=1)
            here = pl.ds(4 * q * b, 4 * q)
            accs = []
            for l in range(3):
                acc = jnp.dot(lhs, w2_ref[i, l], preferred_element_type=F32)
                if i != 1:
                    acc += acc_ref[l, here]
                accs.append(acc)
            if not last:
                for l in range(3):
                    acc_ref[l, here] = accs[l]
                return carry
            col = lax.rem(lax.broadcasted_iota(jnp.int32, (4 * q, k), 0), q)
            left = jnp.where(col == 0, 0.0, pltpu.roll(accs[0], 1, 0))
            right = jnp.where(col == q - 1, 0.0, pltpu.roll(accs[2], 4 * q - 1, 0))
            res = left + accs[1] + right + b2_ref[...]
            out_ref[pl.ds(4 * b, 4)] = res.reshape(4, q, k).astype(BF)
            return carry

        lax.fori_loop(0, mine // 4, rows4, 0)

    @pl.when(slab + 1 < slabs)
    def _():
        low_copy().wait_send()
    for s in range(1, parts):
        for h in range(pieces):
            sum_copy(jnp.int32(s), h).wait_send()
    for n, (dc, ds) in enumerate(AROUND):
        @pl.when(inside(dc, ds))
        def _(n=n):
            halo_copy(n).wait_send()


def local(volume, weight_one, bias_one, weight_two, bias_two):
    c, planes, height, width = volume.shape
    k = weight_one.shape[4]
    parts, slabs = lax.axis_size("chan"), lax.axis_size("slab")
    own_t = volume.transpose(1, 2, 0, 3)
    rows, cols = height // 2, width // 2
    mine = rows // parts
    step = 256 // c if mine % (256 // c) == 0 else mine
    vmem = pl.BlockSpec(memory_space=pltpu.VMEM)
    dma = pltpu.SemaphoreType.DMA
    block = jax.ShapeDtypeStruct((mine, cols, k), BF)
    act, grouped = pl.pallas_call(
        functools.partial(body, parts, slabs),
        out_shape=(block, block),
        in_specs=[vmem] * 5,
        out_specs=(vmem, vmem),
        scratch_shapes=[
            pltpu.VMEM((height, c, width), BF),
            pltpu.VMEM((9, height * c // 128 + 1, cols, 128), BF),
            pltpu.VMEM((rows, cols, k), BF),
            pltpu.VMEM((parts - 1, mine, cols, k), BF),
            pltpu.VMEM((3, mine + 2, cols, k), BF),
            pltpu.VMEM((9 * 256, 64 // c * k), BF),
            pltpu.VMEM((3, 3, 3 * k, k), BF),
            pltpu.VMEM((3, mine * cols, k), F32),
            dma, dma,
            dma((parts - 1, mine // step)), dma((parts - 1, mine // step)),
            dma((8,)), dma((8,)),
        ],
        compiler_params=pltpu.CompilerParams(vmem_limit_bytes=48 << 20, collective_id=0, has_side_effects=True),
    )(own_t, weight_one, bias_one.reshape(1, k), weight_two, bias_two.reshape(1, k))
    return act[None], grouped[None]


def solution(mesh):
    in_specs = (P("chan", "slab", None, None), P(None, None, None, "chan", None), P(), P(), P())
    out_specs = (P("slab", "chan", None, None), P("slab", "chan", None, None))
    return jax.shard_map(local, mesh=mesh, in_specs=in_specs, out_specs=out_specs, check_vma=False)
```

```python
import functools

import jax
import jax.numpy as jnp
from jax import lax
from jax.experimental import pallas as pl
from jax.experimental.pallas import tpu as pltpu
from jax.sharding import PartitionSpec as P

BF = jnp.bfloat16
F32 = jnp.float32
MESH = pl.DeviceIdType.MESH
AROUND = [(0, 1), (0, -1), (1, 0), (-1, 0), (1, 1), (1, -1), (-1, 1), (-1, -1)]


def leaky(value):
    return jnp.where(value > 0, value, 0.3 * value)


def body(parts, slabs, own_ref, k1_ref, b1_ref, k2_ref, b2_ref, act_ref, out_ref,
         low_ref, t_ref, part_ref, recv_ref, a_ref, w1_ref, w2_ref, acc_ref,
         low_send, low_recv, sum_send, sum_recv, halo_send, halo_recv):
    c = own_ref.shape[2]
    tall = 128 // c
    wins = own_ref.shape[1] // tall
    half = own_ref.shape[3] // 2
    mine, q, k = act_ref.shape
    outs = tall // 2
    step = 4 * outs if mine % (4 * outs) == 0 else mine
    pieces = mine // step
    me, slab = lax.axis_index("chan"), lax.axis_index("slab")

    def peer(s):
        if parts == 4:
            return 2 * lax.rem(me // 2 + lax.div(s, 2), 2) + lax.rem(lax.rem(me, 2) + lax.rem(s, 2), 2)
        return lax.rem(me + s, parts)

    def inside(dc, ds):
        ok = None
        for coord, move, size in ((me, dc, parts), (slab, ds, slabs)):
            if move:
                one = coord + move < size if move > 0 else coord + move >= 0
                ok = one if ok is None else jnp.logical_and(ok, one)
        return ok

    barrier = pltpu.get_barrier_semaphore()
    for s in range(1, parts):
        pl.semaphore_signal(barrier, inc=1, device_id={"chan": peer(jnp.int32(s)), "slab": slab}, device_id_type=MESH)
    for dc, ds in AROUND:
        if ds:
            @pl.when(inside(dc, ds))
            def _(dc=dc, ds=ds):
                pl.semaphore_signal(barrier, inc=1, device_id={"chan": me + dc, "slab": slab + ds}, device_id_type=MESH)
    one = jnp.int32(1)
    across = jnp.minimum(slab, one) + jnp.minimum(jnp.int32(slabs - 1) - slab, one)
    along = one + jnp.minimum(me, one) + jnp.minimum(jnp.int32(parts - 1) - me, one)
    pl.semaphore_wait(barrier, jnp.int32(parts - 1) + across * along)

    def low_copy():
        return pltpu.make_async_remote_copy(
            src_ref=own_ref.at[own_ref.shape[0] - 1], dst_ref=low_ref, send_sem=low_send, recv_sem=low_recv,
            device_id={"chan": me, "slab": slab + 1}, device_id_type=MESH)

    @pl.when(slab + 1 < slabs)
    def _():
        low_copy().start()

    w1_ref[...] = jnp.zeros_like(w1_ref)
    for e in range(9):
        i, l = divmod(e, 3)
        for par in range(outs):
            for j in range(3):
                start = e * 256 + (tall - 1 + 2 * par + j) * c
                w1_ref[start:start + c, par * k:(par + 1) * k] = k1_ref[i, j, l]
    m = k2_ref.shape[3]
    group = lax.broadcasted_iota(jnp.int32, (m, k), 1) // m
    for i in range(3):
        for l in range(3):
            for j in range(3):
                taps = k2_ref[i, j, l]
                for g in range(k // m):
                    w2_ref[i, l, j * k + g * m:j * k + (g + 1) * m] = jnp.where(group == g, taps, jnp.zeros_like(taps))
    width = own_ref.shape[3]
    spot = lax.broadcasted_iota(jnp.int32, (half, width), 1) - 2 * lax.broadcasted_iota(jnp.int32, (half, width), 0)
    sel = jnp.concatenate([jnp.where(spot == l - 1, 1.0, 0.0) for l in range(3)], axis=0).astype(BF)
    for e in range(9):
        t_ref[e, 0] = jnp.zeros_like(t_ref[e, 0])

    def decimate(d):
        def go(b, carry):
            rows = pl.ds(4 * tall * b, 4 * tall)
            x = low_ref[rows] if d == 0 else own_ref[d - 1, rows]
            x = x.reshape(512, own_ref.shape[3])
            t = lax.dot_general(sel, x, (((1,), (1,)), ((), ())), preferred_element_type=F32).astype(BF)
            for l in range(3):
                for u in range(4):
                    t_ref[3 * d + l, 4 * b + u + 1] = t[l * half:(l + 1) * half, 128 * u:128 * (u + 1)]
            return carry

        lax.fori_loop(0, wins // 4, go, 0)

    decimate(1)
    decimate(2)

    @pl.when(slab == 0)
    def _():
        low_ref[...] = jnp.zeros_like(low_ref)

    @pl.when(slab > 0)
    def _():
        low_copy().wait_recv()

    decimate(0)

    def chunk(b):
        lhs = []
        for e in range(9):
            lhs.append(t_ref[e, pl.ds(4 * b, 4)].reshape(4 * half, 128))
            lhs.append(t_ref[e, pl.ds(4 * b + 1, 4)].reshape(4 * half, 128))
        res = jnp.dot(jnp.concatenate(lhs, axis=1), w1_ref[...], preferred_element_type=F32).astype(BF)
        for u in range(4):
            for par in range(outs):
                part_ref[4 * outs * b + outs * u + par] = res[u * half:(u + 1) * half, par * k:(par + 1) * k]

    def sum_copy(s, h):
        to = peer(s)
        return pltpu.make_async_remote_copy(
            src_ref=part_ref.at[pl.ds(to * mine + h * step, step)], dst_ref=recv_ref.at[s - 1, pl.ds(h * step, step)],
            send_sem=sum_send.at[s - 1, h], recv_sem=sum_recv.at[s - 1, h],
            device_id={"chan": to, "slab": slab}, device_id_type=MESH)

    if step == 4 * outs:
        def away(n, carry):
            s, h = parts - 1 - lax.rem(n, parts - 1), lax.div(n, parts - 1)
            chunk(peer(s) * pieces + h)
            sum_copy(s, h).start()
            return carry

        def home(h, carry):
            chunk(me * pieces + h)
            return carry

        lax.fori_loop(0, (parts - 1) * pieces, away, 0)
        lax.fori_loop(0, pieces, home, 0)
    else:
        def one(n, carry):
            chunk(n)
            return carry

        lax.fori_loop(0, wins // 4, one, 0)
        for s in range(1, parts):
            sum_copy(jnp.int32(s), 0).start()

    def spots(dc, ds, h):
        if dc == 0:
            rows = pl.ds(1 + h * step, step)
            return a_ref.at[1, rows], a_ref.at[1 - ds, rows]
        return a_ref.at[1, pl.ds(mine if dc > 0 else 1, 1)], a_ref.at[1 - ds, pl.ds(0 if dc > 0 else mine + 1, 1)]

    def halo_copy(n, h):
        dc, ds = AROUND[n]
        src, dst = spots(dc, ds, h)
        return pltpu.make_async_remote_copy(
            src_ref=src, dst_ref=dst, send_sem=halo_send.at[n, h], recv_sem=halo_recv.at[n, h],
            device_id={"chan": me + dc, "slab": slab + ds}, device_id_type=MESH)

    def due(dc):
        return range(pieces) if dc == 0 else (pieces - 1,) if dc > 0 else (0,)

    def arrive(n):
        dc, ds = AROUND[n]
        there = inside(-dc, -ds)
        for h in due(dc):
            @pl.when(there)
            def _(h=h):
                halo_copy(n, h).wait_recv()

            @pl.when(jnp.logical_not(there))
            def _(h=h):
                dst = spots(dc, ds, h)[1]
                dst[...] = jnp.zeros(dst.shape, BF)

    for h in range(pieces):
        for s in range(1, parts):
            sum_copy(jnp.int32(s), h).wait_recv()
        for r in range(h * step, (h + 1) * step, 4):
            total = part_ref[pl.ds(me * mine + r, 4)].astype(F32)
            for s in range(1, parts):
                total += recv_ref[s - 1, r:r + 4].astype(F32)
            act = leaky(total + b1_ref[...]).astype(BF)
            act_ref[r:r + 4] = act
            a_ref[1, r + 1:r + 5] = act
        for n, (dc, ds) in enumerate(AROUND):
            if h in due(dc):
                @pl.when(inside(dc, ds))
                def _(n=n, h=h):
                    halo_copy(n, h).start()

    for i, last in ((1, False), (0, False), (2, True)):
        for n, (dc, ds) in enumerate(AROUND):
            if 1 - ds == i:
                arrive(n)

        def rows4(b, carry, i=i, last=last):
            lhs = jnp.concatenate([a_ref[i, pl.ds(4 * b + j, 4)].reshape(4 * q, k) for j in range(3)], axis=1)
            here = pl.ds(4 * q * b, 4 * q)
            accs = []
            for l in range(3):
                acc = jnp.dot(lhs, w2_ref[i, l], preferred_element_type=F32)
                if i != 1:
                    acc += acc_ref[l, here]
                accs.append(acc)
            if not last:
                for l in range(3):
                    acc_ref[l, here] = accs[l]
                return carry
            col = lax.rem(lax.broadcasted_iota(jnp.int32, (4 * q, k), 0), q)
            left = jnp.where(col == 0, 0.0, pltpu.roll(accs[0], 1, 0))
            right = jnp.where(col == q - 1, 0.0, pltpu.roll(accs[2], 4 * q - 1, 0))
            res = left + accs[1] + right + b2_ref[...]
            out_ref[pl.ds(4 * b, 4)] = res.reshape(4, q, k).astype(BF)
            return carry

        lax.fori_loop(0, mine // 4, rows4, 0)

    @pl.when(slab + 1 < slabs)
    def _():
        low_copy().wait_send()
    for s in range(1, parts):
        for h in range(pieces):
            sum_copy(jnp.int32(s), h).wait_send()
    for n, (dc, ds) in enumerate(AROUND):
        for h in due(dc):
            @pl.when(inside(dc, ds))
            def _(n=n, h=h):
                halo_copy(n, h).wait_send()


def local(volume, weight_one, bias_one, weight_two, bias_two):
    c, planes, height, width = volume.shape
    k = weight_one.shape[4]
    parts, slabs = lax.axis_size("chan"), lax.axis_size("slab")
    own_t = volume.transpose(1, 2, 0, 3)
    rows, cols = height // 2, width // 2
    mine = rows // parts
    step = 256 // c if mine % (256 // c) == 0 else mine
    vmem = pl.BlockSpec(memory_space=pltpu.VMEM)
    dma = pltpu.SemaphoreType.DMA
    block = jax.ShapeDtypeStruct((mine, cols, k), BF)
    act, grouped = pl.pallas_call(
        functools.partial(body, parts, slabs),
        out_shape=(block, block),
        in_specs=[vmem] * 5,
        out_specs=(vmem, vmem),
        scratch_shapes=[
            pltpu.VMEM((height, c, width), BF),
            pltpu.VMEM((9, height * c // 128 + 1, cols, 128), BF),
            pltpu.VMEM((rows, cols, k), BF),
            pltpu.VMEM((parts - 1, mine, cols, k), BF),
            pltpu.VMEM((3, mine + 2, cols, k), BF),
            pltpu.VMEM((9 * 256, 64 // c * k), BF),
            pltpu.VMEM((3, 3, 3 * k, k), BF),
            pltpu.VMEM((3, mine * cols, k), F32),
            dma, dma,
            dma((parts - 1, mine // step)), dma((parts - 1, mine // step)),
            dma((8, mine // step)), dma((8, mine // step)),
        ],
        compiler_params=pltpu.CompilerParams(vmem_limit_bytes=48 << 20, collective_id=0, has_side_effects=True),
    )(own_t, weight_one, bias_one.reshape(1, k), weight_two, bias_two.reshape(1, k))
    return act[None], grouped[None]


def solution(mesh):
    in_specs = (P("chan", "slab", None, None), P(None, None, None, "chan", None), P(), P(), P())
    out_specs = (P("slab", "chan", None, None), P("slab", "chan", None, None))
    return jax.shard_map(local, mesh=mesh, in_specs=in_specs, out_specs=out_specs, check_vma=False)
```

```python
import functools

import jax
import jax.numpy as jnp
from jax import lax
from jax.experimental import pallas as pl
from jax.experimental.pallas import tpu as pltpu
from jax.sharding import PartitionSpec as P

BF = jnp.bfloat16
F32 = jnp.float32
MESH = pl.DeviceIdType.MESH
AROUND = [(0, 1), (0, -1), (1, 0), (-1, 0), (1, 1), (1, -1), (-1, 1), (-1, -1)]


def leaky(value):
    return jnp.where(value > 0, value, 0.3 * value)


def body(parts, slabs, own_ref, k1_ref, b1_ref, k2_ref, b2_ref, act_ref, out_ref,
         low_ref, t_ref, part_ref, recv_ref, a_ref, w1_ref, w2_ref, acc_ref,
         low_send, low_recv, sum_send, sum_recv, halo_send, halo_recv):
    c = own_ref.shape[2]
    tall = 128 // c
    wins = own_ref.shape[1] // tall
    half = own_ref.shape[3] // 2
    mine, q, k = act_ref.shape
    outs = tall // 2
    step = 4 * outs if mine % (4 * outs) == 0 else mine
    pieces = mine // step
    me, slab = lax.axis_index("chan"), lax.axis_index("slab")

    def peer(s):
        if parts == 4:
            return 2 * lax.rem(me // 2 + lax.div(s, 2), 2) + lax.rem(lax.rem(me, 2) + lax.rem(s, 2), 2)
        return lax.rem(me + s, parts)

    def inside(dc, ds):
        ok = None
        for coord, move, size in ((me, dc, parts), (slab, ds, slabs)):
            if move:
                one = coord + move < size if move > 0 else coord + move >= 0
                ok = one if ok is None else jnp.logical_and(ok, one)
        return ok

    barrier = pltpu.get_barrier_semaphore()
    for s in range(1, parts):
        pl.semaphore_signal(barrier, inc=1, device_id={"chan": peer(jnp.int32(s)), "slab": slab}, device_id_type=MESH)
    for dc, ds in AROUND:
        if ds:
            @pl.when(inside(dc, ds))
            def _(dc=dc, ds=ds):
                pl.semaphore_signal(barrier, inc=1, device_id={"chan": me + dc, "slab": slab + ds}, device_id_type=MESH)
    one = jnp.int32(1)
    across = jnp.minimum(slab, one) + jnp.minimum(jnp.int32(slabs - 1) - slab, one)
    along = one + jnp.minimum(me, one) + jnp.minimum(jnp.int32(parts - 1) - me, one)
    pl.semaphore_wait(barrier, jnp.int32(parts - 1) + across * along)

    def low_copy():
        return pltpu.make_async_remote_copy(
            src_ref=own_ref.at[own_ref.shape[0] - 1], dst_ref=low_ref, send_sem=low_send, recv_sem=low_recv,
            device_id={"chan": me, "slab": slab + 1}, device_id_type=MESH)

    @pl.when(slab + 1 < slabs)
    def _():
        low_copy().start()

    w1_ref[...] = jnp.zeros_like(w1_ref)
    for e in range(9):
        i, l = divmod(e, 3)
        for par in range(outs):
            for j in range(3):
                start = e * 256 + (tall - 1 + 2 * par + j) * c
                w1_ref[start:start + c, par * k:(par + 1) * k] = k1_ref[i, j, l]
    m = k2_ref.shape[3]
    group = lax.broadcasted_iota(jnp.int32, (m, k), 1) // m
    for i in range(3):
        for l in range(3):
            for j in range(3):
                taps = k2_ref[i, j, l]
                for g in range(k // m):
                    w2_ref[i, l, j * k + g * m:j * k + (g + 1) * m] = jnp.where(group == g, taps, jnp.zeros_like(taps))
    width = own_ref.shape[3]
    spot = lax.broadcasted_iota(jnp.int32, (half, width), 1) - 2 * lax.broadcasted_iota(jnp.int32, (half, width), 0)
    sel = jnp.concatenate([jnp.where(spot == l - 1, 1.0, 0.0) for l in range(3)], axis=0).astype(BF)
    for e in range(9):
        t_ref[e, 0] = jnp.zeros_like(t_ref[e, 0])

    def decimate(d):
        def go(b, carry):
            rows = pl.ds(4 * tall * b, 4 * tall)
            x = low_ref[rows] if d == 0 else own_ref[d - 1, rows]
            x = x.reshape(512, own_ref.shape[3])
            t = lax.dot_general(sel, x, (((1,), (1,)), ((), ())), preferred_element_type=F32).astype(BF)
            for l in range(3):
                for u in range(4):
                    t_ref[3 * d + l, 4 * b + u + 1] = t[l * half:(l + 1) * half, 128 * u:128 * (u + 1)]
            return carry

        lax.fori_loop(0, wins // 4, go, 0)

    decimate(1)
    decimate(2)

    @pl.when(slab == 0)
    def _():
        low_ref[...] = jnp.zeros_like(low_ref)

    @pl.when(slab > 0)
    def _():
        low_copy().wait_recv()

    decimate(0)

    def chunk(b):
        lhs = []
        for e in range(9):
            lhs.append(t_ref[e, pl.ds(4 * b, 4)].reshape(4 * half, 128))
            lhs.append(t_ref[e, pl.ds(4 * b + 1, 4)].reshape(4 * half, 128))
        res = jnp.dot(jnp.concatenate(lhs, axis=1), w1_ref[...], preferred_element_type=F32).astype(BF)
        for u in range(4):
            for par in range(outs):
                part_ref[4 * outs * b + outs * u + par] = res[u * half:(u + 1) * half, par * k:(par + 1) * k]

    def sum_copy(s, h):
        to = peer(s)
        return pltpu.make_async_remote_copy(
            src_ref=part_ref.at[pl.ds(to * mine + h * step, step)], dst_ref=recv_ref.at[s - 1, pl.ds(h * step, step)],
            send_sem=sum_send.at[s - 1, h], recv_sem=sum_recv.at[s - 1, h],
            device_id={"chan": to, "slab": slab}, device_id_type=MESH)

    paired = parts == 4 and step == 4 * outs
    hop = step // 2

    def stage(slot, h, u):
        to = peer(jnp.int32(1 + u if slot < 2 else 2 - u))
        block = peer(jnp.int32(3)) if slot == 1 else to
        at = h * step + u * hop
        return pltpu.make_async_remote_copy(
            src_ref=part_ref.at[pl.ds(block * mine + at, hop)], dst_ref=recv_ref.at[slot, pl.ds(at, hop)],
            send_sem=sum_send.at[slot, 2 * h + u], recv_sem=sum_recv.at[slot, 2 * h + u],
            device_id={"chan": to, "slab": slab}, device_id_type=MESH)

    if paired:
        far, across_x, across_y = (peer(jnp.int32(s)) for s in (3, 1, 2))

        def first(h, carry):
            chunk(far * pieces + h)
            stage(1, h, 0).start()
            stage(1, h, 1).start()
            chunk(across_x * pieces + h)
            stage(0, h, 0).start()
            chunk(across_y * pieces + h)
            stage(0, h, 1).start()
            return carry

        lax.fori_loop(0, pieces, first, 0)
        for h in range(pieces):
            for u, block in ((0, across_y), (1, across_x)):
                at = h * step + u * hop
                stage(1, h, u).wait_recv()
                here = pl.ds(block * mine + at, hop)
                both = part_ref[here].astype(F32) + recv_ref[1, at:at + hop].astype(F32)
                part_ref[here] = both.astype(BF)
                stage(2, h, u).start()
            chunk(me * pieces + h)
    elif step == 4 * outs:
        def away(n, carry):
            s, h = parts - 1 - lax.rem(n, parts - 1), lax.div(n, parts - 1)
            chunk(peer(s) * pieces + h)
            sum_copy(s, h).start()
            return carry

        def home(h, carry):
            chunk(me * pieces + h)
            return carry

        lax.fori_loop(0, (parts - 1) * pieces, away, 0)
        lax.fori_loop(0, pieces, home, 0)
    else:
        def one(n, carry):
            chunk(n)
            return carry

        lax.fori_loop(0, wins // 4, one, 0)
        for s in range(1, parts):
            sum_copy(jnp.int32(s), 0).start()

    def spots(dc, ds, h):
        if dc == 0:
            rows = pl.ds(1 + h * step, step)
            return a_ref.at[1, rows], a_ref.at[1 - ds, rows]
        return a_ref.at[1, pl.ds(mine if dc > 0 else 1, 1)], a_ref.at[1 - ds, pl.ds(0 if dc > 0 else mine + 1, 1)]

    def halo_copy(n, h):
        dc, ds = AROUND[n]
        src, dst = spots(dc, ds, h)
        return pltpu.make_async_remote_copy(
            src_ref=src, dst_ref=dst, send_sem=halo_send.at[n, h], recv_sem=halo_recv.at[n, h],
            device_id={"chan": me + dc, "slab": slab + ds}, device_id_type=MESH)

    def due(dc):
        return range(pieces) if dc == 0 else (pieces - 1,) if dc > 0 else (0,)

    def arrive(n):
        dc, ds = AROUND[n]
        there = inside(-dc, -ds)
        for h in due(dc):
            @pl.when(there)
            def _(h=h):
                halo_copy(n, h).wait_recv()

            @pl.when(jnp.logical_not(there))
            def _(h=h):
                dst = spots(dc, ds, h)[1]
                dst[...] = jnp.zeros(dst.shape, BF)

    for h in range(pieces):
        for slot in (0, 2) if paired else ():
            stage(slot, h, 0).wait_recv()
            stage(slot, h, 1).wait_recv()
        for s in () if paired else range(1, parts):
            sum_copy(jnp.int32(s), h).wait_recv()
        for r in range(h * step, (h + 1) * step, 4):
            total = part_ref[pl.ds(me * mine + r, 4)].astype(F32)
            for slot in (0, 2) if paired else range(parts - 1):
                total += recv_ref[slot, r:r + 4].astype(F32)
            act = leaky(total + b1_ref[...]).astype(BF)
            act_ref[r:r + 4] = act
            a_ref[1, r + 1:r + 5] = act
        for n, (dc, ds) in enumerate(AROUND):
            if h in due(dc):
                @pl.when(inside(dc, ds))
                def _(n=n, h=h):
                    halo_copy(n, h).start()

    for i, last in ((1, False), (0, False), (2, True)):
        for n, (dc, ds) in enumerate(AROUND):
            if 1 - ds == i:
                arrive(n)

        def rows4(b, carry, i=i, last=last):
            lhs = jnp.concatenate([a_ref[i, pl.ds(4 * b + j, 4)].reshape(4 * q, k) for j in range(3)], axis=1)
            here = pl.ds(4 * q * b, 4 * q)
            accs = []
            for l in range(3):
                acc = jnp.dot(lhs, w2_ref[i, l], preferred_element_type=F32)
                if i != 1:
                    acc += acc_ref[l, here]
                accs.append(acc)
            if not last:
                for l in range(3):
                    acc_ref[l, here] = accs[l]
                return carry
            col = lax.rem(lax.broadcasted_iota(jnp.int32, (4 * q, k), 0), q)
            left = jnp.where(col == 0, 0.0, pltpu.roll(accs[0], 1, 0))
            right = jnp.where(col == q - 1, 0.0, pltpu.roll(accs[2], 4 * q - 1, 0))
            res = left + accs[1] + right + b2_ref[...]
            out_ref[pl.ds(4 * b, 4)] = res.reshape(4, q, k).astype(BF)
            return carry

        lax.fori_loop(0, mine // 4, rows4, 0)

    @pl.when(slab + 1 < slabs)
    def _():
        low_copy().wait_send()
    for s in range(1, parts):
        for h in range(pieces):
            if paired:
                stage(s - 1, h, 0).wait_send()
                stage(s - 1, h, 1).wait_send()
            else:
                sum_copy(jnp.int32(s), h).wait_send()
    for n, (dc, ds) in enumerate(AROUND):
        for h in due(dc):
            @pl.when(inside(dc, ds))
            def _(n=n, h=h):
                halo_copy(n, h).wait_send()


def local(volume, weight_one, bias_one, weight_two, bias_two):
    c, planes, height, width = volume.shape
    k = weight_one.shape[4]
    parts, slabs = lax.axis_size("chan"), lax.axis_size("slab")
    own_t = volume.transpose(1, 2, 0, 3)
    rows, cols = height // 2, width // 2
    mine = rows // parts
    step = 256 // c if mine % (256 // c) == 0 else mine
    vmem = pl.BlockSpec(memory_space=pltpu.VMEM)
    dma = pltpu.SemaphoreType.DMA
    block = jax.ShapeDtypeStruct((mine, cols, k), BF)
    act, grouped = pl.pallas_call(
        functools.partial(body, parts, slabs),
        out_shape=(block, block),
        in_specs=[vmem] * 5,
        out_specs=(vmem, vmem),
        scratch_shapes=[
            pltpu.VMEM((height, c, width), BF),
            pltpu.VMEM((9, height * c // 128 + 1, cols, 128), BF),
            pltpu.VMEM((rows, cols, k), BF),
            pltpu.VMEM((parts - 1, mine, cols, k), BF),
            pltpu.VMEM((3, mine + 2, cols, k), BF),
            pltpu.VMEM((9 * 256, 64 // c * k), BF),
            pltpu.VMEM((3, 3, 3 * k, k), BF),
            pltpu.VMEM((3, mine * cols, k), F32),
            dma, dma,
            dma((parts - 1, 2 * mine // step)), dma((parts - 1, 2 * mine // step)),
            dma((8, mine // step)), dma((8, mine // step)),
        ],
        compiler_params=pltpu.CompilerParams(vmem_limit_bytes=48 << 20, collective_id=0, has_side_effects=True),
    )(own_t, weight_one, bias_one.reshape(1, k), weight_two, bias_two.reshape(1, k))
    return act[None], grouped[None]


def solution(mesh):
    in_specs = (P("chan", "slab", None, None), P(None, None, None, "chan", None), P(), P(), P())
    out_specs = (P("slab", "chan", None, None), P("slab", "chan", None, None))
    return jax.shard_map(local, mesh=mesh, in_specs=in_specs, out_specs=out_specs, check_vma=False)
```
